32 devices in a mesh: seq: 8 (over z, core), head: 4 (over y, x).
Axes of the slice: x: 2, y: 2, z: 4, core: 2. Of those that a mesh axis runs over, the one named last changes fastest.
Arguments:
- tokens: bfloat16 [4096, 2304], P(('seq', 'head')), may hold values from -6 to 6
- in_gain: float32 [2304], replicated, may hold values from 0.5 to 1.5
- out_gain: float32 [2304], replicated, may hold values from 0.5 to 1.5
- query_weight: bfloat16 [2304, 2048], P(None, 'head'), may hold values from -1.25 to 1.25
- keyval_weight: bfloat16 [2304, 2048], replicated, may hold values from -0.125 to 0.125
- out_weight: bfloat16 [2048, 2304], P('head'), may hold values from -0.125 to 0.125
- cache_entries: bfloat16 [4, 2048, 512], P(None, 'seq'), may hold values from -6 to 6
- segment_ids: int32 [4096], P('seq'), may hold values from -1 to 63, as said below
- cache_lengths: int32 [64], replicated, may hold values from 0 to 512, as said below
- block_owners: int32 [128], P('seq'), may hold values from -1 to 63, as said below
Outputs:
- layer_out: bfloat16 [4096, 2304], P(('seq', 'head'))
The draws below stay inside these ranges and needn't reach their ends.
Inputs may be any that keep to these rules, and one draw needn't show every extreme that they name: `segment_ids`: valid slots come first and their ids never fall; every id from 0 to 63 has at least one slot; padding slots, marked -1, fill the end of the stream; exactly one segment has 2048 slots and none has more. `block_owners`: the segment that owns each cache block, or -1 for a free block; a segment's cache fills its blocks in the order of their indices; no segment owns more than 32 blocks. `cache_lengths`: zero for a segment without blocks, and some segment has none; otherwise more than 16 times one less than its number of blocks and at most 16 times that number; exactly one segment holds 512 rows.
All inputs are finite; a program needn't handle non-finite values.
Results may differ from the reference program's by a relative error of at most 0.012.
Values may be sent and summed in bfloat16 or wider, within the bound.
A program may use at most 128 MiB of HBM per device.

```python
import math
import jax
import jax.numpy as jnp
from jax import lax

D = 2304
QH = 8
KVH = 4
HD = 256
NSEG = 64
BLK = 16
TOKENS = 4096
CACHE_ROWS = 2048
CBLK = 128
MAXSEG = 2048


def segment_plan(key):
    pad_key, long_key, weight_key = jax.random.split(key, 3)
    padding = jax.random.randint(pad_key, (), 0, TOKENS // 16 + 1)
    longest = jax.random.randint(long_key, (), 0, NSEG)
    seg_range = jnp.arange(NSEG, dtype=jnp.int32)
    weights = jax.random.randint(weight_key, (NSEG,), 1, 100)
    weights = jnp.where(seg_range == longest, 0, weights)
    remainder = TOKENS - padding - MAXSEG - (NSEG - 1)
    surplus = remainder * weights // jnp.sum(weights)
    leftover = remainder - jnp.sum(surplus)
    receiver = (longest + 1) % NSEG
    lengths = jnp.where(seg_range == longest, MAXSEG, 1 + surplus + jnp.where(seg_range == receiver, leftover, 0))
    return (lengths.astype(jnp.int32), padding)


def draw_segment_ids(key, part):
    lengths, padding = segment_plan(jax.random.fold_in(key, 11))
    boundaries = jnp.cumsum(lengths)
    slot_index = jnp.arange(TOKENS, dtype=jnp.int32)
    labels = jnp.sum((slot_index[:, None] >= boundaries[None, :]).astype(jnp.int32), axis=1)
    return jnp.where(slot_index < TOKENS - padding, labels, -1).astype(jnp.int32)


def cache_plan(key):
    perm_key, heavy_key, empty_key, free_key, fill_key = jax.random.split(jax.random.fold_in(key, 23), 5)
    without = jax.random.randint(empty_key, (), 0, NSEG)
    heavy = (without + 1 + jax.random.randint(heavy_key, (), 0, NSEG - 1)) % NSEG
    block_index = jnp.arange(CBLK, dtype=jnp.int32)
    group = block_index // 4
    within = block_index % 4
    cycle = (3 * group + within - 1) % NSEG
    order = jax.random.permutation(perm_key, NSEG).astype(jnp.int32)
    owners = jnp.take(order, cycle)
    freed = jax.random.randint(free_key, (CBLK,), 0, 4) == 0
    owners = jnp.where(freed | (owners == heavy) | (owners == without), -1, owners)
    owners = jnp.where(within == 0, heavy, owners)
    seg_range = jnp.arange(NSEG, dtype=jnp.int32)
    owned_count = jnp.sum((owners[:, None] == seg_range[None, :]).astype(jnp.int32), axis=0)
    partial_value = jax.random.randint(fill_key, (NSEG,), 1, BLK + 1)
    partial_value = jnp.where(seg_range == heavy, BLK, partial_value)
    lengths = jnp.where(owned_count > 0, BLK * (owned_count - 1) + partial_value, 0)
    return (owners.astype(jnp.int32), lengths.astype(jnp.int32))


def draw_block_owners(key, part):
    owners, lengths = cache_plan(key)
    return owners


def draw_cache_lengths(key, part):
    owners, lengths = cache_plan(key)
    return lengths


def levels(rng, shape, cuts, least, largest):
    gain = 1.0
    for dim, shards_of in cuts:
        draws = jax.random.uniform(jax.random.fold_in(jax.random.fold_in(rng, 6), dim), (shards_of,), jnp.float32, least / len(cuts), largest / len(cuts))
        gain = gain * jnp.repeat(jnp.exp(draws), shape[dim] // shards_of).reshape((-1,) + (1,) * (len(shape) - 1 - dim))
    return gain


def noise(own_key, shape, scale, bound, shards=(), kind=jnp.bfloat16):
    array = jax.random.normal(own_key, shape, jnp.float32) * scale
    if len(shards) > 0:
        array = levels(own_key, shape, shards, -0.22, 0.18) * array
    return jnp.clip(array, min=-bound, max=bound).astype(kind)


def setup_inputs(seed: int = 0) -> dict:
    seeds = jax.random.split(jax.random.key(seed), 11)
    tokens = noise(seeds[0], (TOKENS, D), 1.0, 6.0, ((0, 32),))
    in_gain = jnp.clip(1.0 + 0.1 * jax.random.normal(seeds[1], (D,), jnp.float32), 0.5, 1.5)
    out_gain = jnp.clip(1.0 + 0.1 * jax.random.normal(seeds[2], (D,), jnp.float32), 0.5, 1.5)
    query_weight = noise(seeds[3], (D, QH * HD), (max(D // 100, 1)) ** -0.5, 1.25, ((1, 4),))
    keyval_weight = noise(seeds[4], (D, KVH * 2 * HD), D ** -0.5, 0.125)
    out_weight = noise(seeds[5], (QH * HD, D), (QH * HD) ** -0.5, 0.125, ((0, 4),))
    cache_entries = noise(seeds[6], (KVH, CACHE_ROWS, 2 * HD), 1.0, 6.0, ((1, 8),))
    segment_ids = draw_segment_ids(jax.random.fold_in(seeds[10], 71), 0)
    cache_lengths = draw_cache_lengths(jax.random.fold_in(seeds[10], 71), 0)
    block_owners = draw_block_owners(jax.random.fold_in(seeds[10], 71), 0)
    return dict(tokens=tokens, in_gain=in_gain, out_gain=out_gain, query_weight=query_weight, keyval_weight=keyval_weight, out_weight=out_weight, cache_entries=cache_entries, segment_ids=segment_ids, cache_lengths=cache_lengths, block_owners=block_owners)


EPSILON = 1e-06
SOFT_CAP = 50.0
far_away = 1073741824

def rms_scale(matrix, scaling):
    matrix = matrix.astype(jnp.float32)
    mean_square = lax.optimization_barrier(jnp.mean(matrix * matrix, axis=-1, keepdims=True))
    return matrix * lax.rsqrt(mean_square + EPSILON) * scaling.astype(jnp.float32)

def frequencies(extent):
    return 10000.0 ** (-(jnp.arange(extent // 2, dtype=jnp.float32) * 2.0 / extent))

def rotate(vectors, angles):
    half_width = vectors.shape[-1] // 2
    leading = vectors[..., :half_width]
    trailing = vectors[..., half_width:]
    cosine = jnp.cos(angles)
    sine_part = jnp.sin(angles)
    return jnp.concatenate([leading * cosine - trailing * sine_part, trailing * cosine + leading * sine_part], axis=-1)

def attend(queries, q_seg, q_slot, key_table, value_table, k_seg, k_slot):
    q_total, head_count, extent = queries.shape
    q_rows = math.gcd(q_total, 1024)
    k_rows = math.gcd(key_table.shape[0], 1024)
    key_blocks = (key_table.reshape(-1, k_rows, extent), value_table.reshape(-1, k_rows, extent), k_seg.reshape(-1, k_rows), k_slot.reshape(-1, k_rows))

    def one_block(query_block):
        query_rows, query_seg, query_slot = query_block
        present = query_seg >= 0
        lowest = jnp.min(jnp.where(present, query_seg, far_away))
        highest = jnp.max(query_seg)
        latest = jnp.max(query_slot)

        def advance(totals, key_block):
            key_rows, value_rows, key_seg, key_slot = key_block

            def accumulate(partial_value):
                numerator, denominator = partial_value
                scores = jnp.einsum('qhd,kd->qhk', query_rows.astype(jnp.float32), key_rows.astype(jnp.float32))
                scores = SOFT_CAP * jnp.tanh(scores / SOFT_CAP)
                allowed = (key_seg[None, :] == query_seg[:, None]) & (key_slot[None, :] <= query_slot[:, None]) & present[:, None]
                weights = jnp.where(allowed[:, None, :], jnp.exp(scores), 0.0)
                rounded = lax.optimization_barrier(weights.astype(jnp.bfloat16))
                numerator = numerator + jnp.einsum('qhk,kd->qhd', rounded.astype(jnp.float32), value_rows.astype(jnp.float32))
                denominator = denominator + lax.optimization_barrier(jnp.sum(weights, axis=-1))
                return (numerator, denominator)
            key_present = key_seg >= 0
            touches = (lowest <= jnp.max(key_seg)) & (jnp.min(jnp.where(key_present, key_seg, far_away)) <= highest) & (jnp.min(key_slot) <= latest)
            return (lax.cond(touches, accumulate, lambda unchanged: unchanged, totals), None)
        start_totals = (jnp.zeros((q_rows, head_count, extent), jnp.float32), jnp.zeros((q_rows, head_count), jnp.float32))
        (numerator, denominator), _ = lax.scan(advance, start_totals, key_blocks)
        safe = jnp.where(present[:, None], denominator, 1.0)
        return jnp.where(present[:, None, None], numerator / safe[:, :, None], 0.0)
    results = lax.map(one_block, (queries.reshape(-1, q_rows, head_count, extent), q_seg.reshape(-1, q_rows), q_slot.reshape(-1, q_rows)))
    return results.reshape(q_total, head_count, extent)

def reference(tokens, in_gain, out_gain, query_weight, keyval_weight, out_weight, cache_entries, segment_ids, cache_lengths, block_owners):
    seg_range = jnp.arange(NSEG, dtype=jnp.int32)
    matches = (segment_ids[:, None] == seg_range[None, :]).astype(jnp.int32)
    counts = lax.optimization_barrier(jnp.sum(matches, axis=0))
    firsts = jnp.cumsum(counts) - counts
    slot_index = jnp.arange(TOKENS, dtype=jnp.int32)
    positions = lax.optimization_barrier(jnp.sum(matches * (cache_lengths - firsts)[None, :], axis=1)) + slot_index
    angles = positions.astype(jnp.float32)[:, None] * frequencies(HD)[None, :]
    normed = rms_scale(tokens, in_gain).astype(jnp.bfloat16)
    projected = jnp.dot(normed, query_weight, preferred_element_type=jnp.float32).reshape(TOKENS, QH, HD)
    queries = lax.optimization_barrier((rotate(projected, angles[:, None, :]) * HD ** (-0.5)).astype(jnp.bfloat16))
    keyvals = jnp.dot(normed, keyval_weight, preferred_element_type=jnp.float32).reshape(TOKENS, KVH, 2 * HD)
    new_keys = lax.optimization_barrier(rotate(keyvals[:, :, :HD], angles[:, None, :]).astype(jnp.bfloat16))
    new_values = lax.optimization_barrier(keyvals[:, :, HD:].astype(jnp.bfloat16))
    owner_match = (block_owners[:, None] == seg_range[None, :]).astype(jnp.int32)
    block_rank = lax.optimization_barrier(jnp.sum(owner_match * (jnp.cumsum(owner_match, axis=0) - owner_match), axis=1))
    limits = lax.optimization_barrier(jnp.sum(owner_match * cache_lengths[None, :], axis=1))
    offsets = jnp.arange(BLK, dtype=jnp.int32)
    usable = (block_owners[:, None] >= 0) & (block_rank[:, None] * BLK + offsets[None, :] < limits[:, None])
    cache_seg = jnp.where(usable, block_owners[:, None], -1).reshape(CACHE_ROWS).astype(jnp.int32)
    key_seg = jnp.concatenate([segment_ids, cache_seg])
    key_slot = jnp.concatenate([slot_index, jnp.full((CACHE_ROWS,), -1, jnp.int32)])
    group_size = QH // KVH
    outputs = []
    for shared in range(KVH):
        key_table = jnp.concatenate([new_keys[:, shared], cache_entries[shared, :, :HD]], axis=0)
        value_table = jnp.concatenate([new_values[:, shared], cache_entries[shared, :, HD:]], axis=0)
        outputs.append(attend(queries[:, shared * group_size:(shared + 1) * group_size], segment_ids, slot_index, key_table, value_table, key_seg, key_slot))
    attended = jnp.stack(outputs, axis=1).astype(jnp.bfloat16).reshape(TOKENS, QH * HD)
    branch = jnp.dot(attended, out_weight, preferred_element_type=jnp.float32)
    return (tokens.astype(jnp.float32) + rms_scale(branch, out_gain)).astype(jnp.bfloat16)
```

```python
import functools
import math

import jax
import jax.numpy as jnp
from jax import lax
from jax.experimental import pallas as pl
from jax.experimental.pallas import tpu as pltpu
from jax.sharding import PartitionSpec as P

QH = 8
KVH = 4
HD = 256
NSEG = 64
BLK = 16
LANES = 128
EPSILON = 1e-06
SOFT_CAP = 50.0
FAR = 1073741824
VMEM_BYTES = 40 << 20


def rms_scale(matrix, scaling):
    matrix = matrix.astype(jnp.float32)
    mean_square = jnp.mean(matrix * matrix, axis=-1, keepdims=True)
    return matrix * lax.rsqrt(mean_square + EPSILON) * scaling


def frequencies(extent):
    return 10000.0 ** (-(jnp.arange(extent // 2, dtype=jnp.float32) * 2.0 / extent))


def project_kernel(heads, which, x_ref, wq_ref, wkv_ref, cos_ref, sin_ref, q_ref, kv_ref):
    half = HD // 2
    x = x_ref[...]
    cosine, sine = cos_ref[...], sin_ref[...]
    for h in range(heads):
        y = jnp.dot(x, wq_ref[:, h * HD : (h + 1) * HD], preferred_element_type=jnp.float32)
        a, b = y[:, :half], y[:, half:]
        q_ref[h, :, :half] = ((a * cosine - b * sine) * HD**-0.5).astype(q_ref.dtype)
        q_ref[h, :, half:] = ((b * cosine + a * sine) * HD**-0.5).astype(q_ref.dtype)
    y = jnp.dot(x, wkv_ref[...], preferred_element_type=jnp.float32)
    a, b = y[:, :half], y[:, half:HD]
    kv_ref[:, :half] = (a * cosine - b * sine).astype(kv_ref.dtype)
    kv_ref[:, half:HD] = (b * cosine + a * sine).astype(kv_ref.dtype)
    kv_ref[:, HD:] = y[:, HD:].astype(kv_ref.dtype)


def project(normed, query_weight, keyval_weight, shared_head, cosine, sine):
    rows, width = normed.shape
    heads = query_weight.shape[1] // HD
    tile = math.gcd(rows, 256)
    return pl.pallas_call(
        functools.partial(project_kernel, heads),
        grid_spec=pltpu.PrefetchScalarGridSpec(
            num_scalar_prefetch=1,
            grid=(rows // tile,),
            in_specs=[
                pl.BlockSpec((tile, width), lambda i, s: (i, 0)),
                pl.BlockSpec((width, heads * HD), lambda i, s: (0, 0)),
                pl.BlockSpec((width, 2 * HD), lambda i, s: (0, s[0])),
                pl.BlockSpec((tile, HD // 2), lambda i, s: (i, 0)),
                pl.BlockSpec((tile, HD // 2), lambda i, s: (i, 0)),
            ],
            out_specs=[
                pl.BlockSpec((heads, tile, HD), lambda i, s: (0, i, 0)),
                pl.BlockSpec((tile, 2 * HD), lambda i, s: (i, 0)),
            ],
        ),
        out_shape=[
            jax.ShapeDtypeStruct((heads, rows, HD), jnp.bfloat16),
            jax.ShapeDtypeStruct((rows, 2 * HD), jnp.bfloat16),
        ],
        compiler_params=pltpu.CompilerParams(vmem_limit_bytes=VMEM_BYTES),
        cost_estimate=pl.CostEstimate(
            flops=2 * rows * width * (heads + 2) * HD,
            bytes_accessed=2 * width * (heads + 2) * HD + 2 * rows * width,
            transcendentals=0,
        ),
        name="project",
    )(shared_head.reshape(1), normed, query_weight, keyval_weight, cosine, sine)


def fold_blocks(
    heads, q_tile, k_tile, touch_ref, q_ref, qseg_ref, qslot_ref, kseg_ref, kslot_ref, parts, acc, den
):
    q_tiles = q_ref.shape[1] // q_tile
    blocks = kseg_ref.shape[0]
    first = 0
    for part in parts:
        here = part.shape[0] // k_tile

        def step(index, carry, part=part, here=here, first=first):
            qi = index // here
            kj = index % here

            @pl.when(touch_ref[qi * blocks + first + kj] > 0)
            def _():
                rows = pl.ds(pl.multiple_of(qi * q_tile, q_tile), q_tile)
                keys = pl.ds(pl.multiple_of(kj * k_tile, k_tile), k_tile)
                allowed = (kseg_ref[first + kj] == qseg_ref[rows, :]) & (
                    kslot_ref[first + kj] <= qslot_ref[rows, :]
                )
                for h in range(heads):
                    scores = lax.dot_general(
                        q_ref[h, rows, :],
                        part[keys, :HD],
                        (((1,), (1,)), ((), ())),
                        preferred_element_type=jnp.float32,
                    )
                    scores = jnp.tanh(scores * (1.0 / SOFT_CAP))
                    weights = jnp.where(
                        allowed, jnp.exp2(scores * (SOFT_CAP * math.log2(math.e))), 0.0
                    )
                    total = weights[:, :LANES]
                    for c in range(1, k_tile // LANES):
                        total += weights[:, c * LANES : (c + 1) * LANES]
                    den[h, rows, :] += total
                    acc[h, rows, :] += jnp.dot(
                        weights.astype(jnp.bfloat16),
                        part[keys, HD:],
                        preferred_element_type=jnp.float32,
                    )

            return carry

        lax.fori_loop(0, q_tiles * here, step, 0)
        first += here


def first_kernel(heads, q_tile, k_tile, count, touch_ref, q_ref, qseg_ref, qslot_ref, kseg_ref, kslot_ref, *rest):
    parts, (acc, den) = rest[:count], rest[count:]
    acc[...] = jnp.zeros_like(acc)
    den[...] = jnp.zeros_like(den)
    fold_blocks(
        heads, q_tile, k_tile, touch_ref, q_ref, qseg_ref, qslot_ref, kseg_ref, kslot_ref, parts, acc, den
    )


def last_kernel(heads, q_tile, k_tile, count, touch_ref, q_ref, qseg_ref, qslot_ref, kseg_ref, kslot_ref, *rest):
    parts, (acc_in, den_in, out_ref, acc, den) = rest[:count], rest[count:]
    acc[...] = acc_in[...]
    den[...] = den_in[...]
    fold_blocks(
        heads, q_tile, k_tile, touch_ref, q_ref, qseg_ref, qslot_ref, kseg_ref, kslot_ref, parts, acc, den
    )
    present = qseg_ref[...] >= 0
    for h in range(heads):
        total = jnp.sum(den[h], axis=-1, keepdims=True)
        safe = jnp.where(present, total, 1.0)
        out_ref[:, h * HD : (h + 1) * HD] = jnp.where(present, acc[h] / safe, 0.0).astype(
            out_ref.dtype
        )


def attend(queries, q_seg, q_slot, parts, k_seg, k_slot, totals=None):
    heads, rows, _ = queries.shape
    q_tile = math.gcd(rows, 256)
    k_tile = math.gcd(*[part.shape[0] for part in parts], 512)
    blocks = k_seg.shape[0] // k_tile
    seg_tiles = q_seg.reshape(-1, q_tile)
    lowest = jnp.min(jnp.where(seg_tiles >= 0, seg_tiles, FAR), axis=1)[:, None]
    highest = jnp.max(seg_tiles, axis=1)[:, None]
    latest = jnp.max(q_slot.reshape(-1, q_tile), axis=1)[:, None]
    near = (k_seg[None] >= lowest) & (k_seg[None] <= highest) & (k_slot[None] <= latest)
    touch = jnp.max(near.astype(jnp.int32).reshape(-1, blocks, k_tile), axis=2).reshape(-1)
    operands = [
        touch,
        queries,
        q_seg[:, None],
        q_slot[:, None],
        k_seg.reshape(blocks, 1, k_tile),
        k_slot.reshape(blocks, 1, k_tile),
        *parts,
    ]
    vmem = pl.BlockSpec(memory_space=pltpu.VMEM)
    sums = [
        jax.ShapeDtypeStruct((heads, rows, HD), jnp.float32),
        jax.ShapeDtypeStruct((heads, rows, LANES), jnp.float32),
    ]
    if totals is None:
        body, out_shape, out_specs, scratch = first_kernel, sums, [vmem, vmem], []
    else:
        operands += list(totals)
        body = last_kernel
        out_shape = jax.ShapeDtypeStruct((rows, heads * HD), jnp.bfloat16)
        out_specs = vmem
        scratch = [pltpu.VMEM(s.shape, s.dtype) for s in sums]
    pairs = heads * rows * k_seg.shape[0]
    return pl.pallas_call(
        functools.partial(body, heads, q_tile, k_tile, len(parts)),
        in_specs=[pl.BlockSpec(memory_space=pltpu.SMEM)] + [vmem] * (len(operands) - 1),
        out_specs=out_specs,
        out_shape=out_shape,
        scratch_shapes=scratch,
        compiler_params=pltpu.CompilerParams(vmem_limit_bytes=VMEM_BYTES),
        cost_estimate=pl.CostEstimate(
            flops=4 * pairs * HD, bytes_accessed=4 * HD * k_seg.shape[0], transcendentals=2 * pairs
        ),
        name="attend",
    )(*operands)


def local(
    tokens,
    in_gain,
    out_gain,
    query_weight,
    keyval_weight,
    out_weight,
    cache_entries,
    segment_ids,
    cache_lengths,
    block_owners,
):
    heads_here = query_weight.shape[1] // HD
    group_size = QH // KVH
    seq_size, head_size = lax.axis_size("seq"), lax.axis_size("head")
    seq_index = lax.axis_index("seq")
    head_index = lax.axis_index("head")
    shared_head = head_index * heads_here // group_size
    stream_rows = segment_ids.shape[0]
    own_rows = tokens.shape[0]
    square = head_size == 4

    def across(array, bits):
        return lax.ppermute(array, "head", [(h, h ^ bits) for h in range(head_size)])

    def relative(array):
        if not square:
            return array
        array = array.reshape(-1, 2, 2, own_rows)
        array = jnp.where(head_index % 2 == 1, array[:, :, ::-1], array)
        array = jnp.where(head_index // 2 == 1, array[:, ::-1], array)
        return array.reshape(-1)

    normed_own = rms_scale(tokens, in_gain).astype(jnp.bfloat16)
    if square:
        half = own_rows // 2
        from_x = across(normed_own, 1)
        from_y = across(normed_own, 2)
        diag_top = across(from_x[:half], 2)
        diag_bottom = across(from_y[half:], 1)
        normed = jnp.concatenate([normed_own, from_x, from_y, diag_top, diag_bottom], axis=0)
    else:
        normed = lax.all_gather(normed_own, "head", axis=0, tiled=True)

    cache_own = lax.dynamic_index_in_dim(cache_entries, shared_head, 0, keepdims=False)
    cache_pairs = lax.all_gather(cache_own, "seq", axis=0, tiled=True)

    table = lax.all_gather(jnp.concatenate([segment_ids, block_owners]), "seq", axis=0)
    seg_all = table[:, :stream_rows].reshape(-1)
    owners = table[:, stream_rows:].reshape(-1)

    seg_range = jnp.arange(NSEG, dtype=jnp.int32)
    earlier = (seg_all[None, :] >= 0) & (seg_all[None, :] < seg_range[:, None])
    firsts = jnp.sum(earlier.astype(jnp.int32), axis=1)
    slots_all = jnp.arange(seg_all.shape[0], dtype=jnp.int32)
    seg_all, slots_all = relative(seg_all), relative(slots_all)
    begin = seq_index * stream_rows
    q_seg = lax.dynamic_slice_in_dim(seg_all, begin, stream_rows)
    q_slot = lax.dynamic_slice_in_dim(slots_all, begin, stream_rows)
    matches = (q_seg[:, None] == seg_range[None, :]).astype(jnp.int32)
    positions = jnp.sum(matches * (cache_lengths - firsts)[None, :], axis=1) + q_slot
    angles = positions.astype(jnp.float32)[:, None] * frequencies(HD)[None, :]
    cosine, sine = jnp.cos(angles), jnp.sin(angles)

    block_index = jnp.arange(owners.shape[0], dtype=jnp.int32)
    same = (owners[:, None] == owners[None, :]) & (block_index[None, :] < block_index[:, None])
    block_rank = jnp.sum(same.astype(jnp.int32), axis=1)
    owner_match = (owners[:, None] == seg_range[None, :]).astype(jnp.int32)
    limits = jnp.sum(owner_match * cache_lengths[None, :], axis=1)
    offsets = jnp.arange(BLK, dtype=jnp.int32)
    usable = (owners[:, None] >= 0) & (
        block_rank[:, None] * BLK + offsets[None, :] < limits[:, None]
    )
    cache_seg = jnp.where(usable, owners[:, None], -2).reshape(-1)
    cache_slot = jnp.full((cache_seg.shape[0],), -1, jnp.int32)

    queries, pairs = project(normed, query_weight, keyval_weight, shared_head, cosine, sine)

    hops = seq_size // 4

    def onward(array):
        return lax.ppermute(array, "seq", [(s, s + 2) for s in range(seq_size - 2)])

    def sibling(array):
        return lax.ppermute(array, "seq", [(s, s ^ 1) for s in range(seq_size)])

    key_seg = jnp.where(seg_all >= 0, seg_all, -2)

    def shard_ints(shard):
        inside = (shard >= 0) & (shard < seq_size)
        at = jnp.clip(shard, 0, seq_size - 1) * stream_rows
        seg = lax.dynamic_slice_in_dim(key_seg, at, stream_rows)
        return jnp.where(inside, seg, -2), lax.dynamic_slice_in_dim(slots_all, at, stream_rows)

    mate = seq_index + 1 - 2 * (seq_index % 2)
    travelling = pairs
    far_parts, far_shards = [], []
    for hop in range(1, hops + 1):
        travelling = onward(travelling)
        far_parts += [travelling, sibling(travelling)]
        far_shards += [seq_index - 2 * hop, mate - 2 * hop]
    near_parts, near_shards = [pairs, sibling(pairs)], [seq_index, mate]

    near_ints = [shard_ints(s) for s in near_shards] + [(cache_seg, cache_slot)]
    far_ints = [shard_ints(s) for s in far_shards]
    totals = attend(
        queries,
        q_seg,
        q_slot,
        near_parts + [cache_pairs],
        jnp.concatenate([i[0] for i in near_ints]),
        jnp.concatenate([i[1] for i in near_ints]),
    )
    attended = attend(
        queries,
        q_seg,
        q_slot,
        far_parts,
        jnp.concatenate([i[0] for i in far_ints]),
        jnp.concatenate([i[1] for i in far_ints]),
        totals,
    )

    if square:
        r = own_rows
        c = out_weight.shape[1] // 2
        left = jnp.dot(attended, out_weight[:, :c], preferred_element_type=jnp.float32)
        right = jnp.dot(attended, out_weight[:, c:], preferred_element_type=jnp.float32)
        wire = jnp.bfloat16
        send_l = jnp.concatenate([left[r : 2 * r], left[3 * r :]]).astype(wire)
        got_l = across(send_l, 1).astype(jnp.float32)
        got_r = across(right[2 * r :].astype(wire), 2).astype(jnp.float32)
        last_l = across((left[2 * r : 3 * r] + got_l[r:]).astype(wire), 2)
        last_r = across((right[r : 2 * r] + got_r[r:]).astype(wire), 1)
        branch = jnp.concatenate(
            [
                left[:r] + got_l[:r] + last_l.astype(jnp.float32),
                right[:r] + got_r[:r] + last_r.astype(jnp.float32),
            ],
            axis=1,
        )
    else:
        branch = lax.psum_scatter(
            jnp.dot(attended, out_weight, preferred_element_type=jnp.float32),
            "head",
            scatter_dimension=0,
            tiled=True,
        )
    return (tokens.astype(jnp.float32) + rms_scale(branch, out_gain)).astype(jnp.bfloat16)


def solution(mesh):
    in_specs = (
        P(("seq", "head"), None),
        P(),
        P(),
        P(None, "head"),
        P(),
        P("head", None),
        P(None, "seq", None),
        P("seq"),
        P(),
        P("seq"),
    )
    out_specs = P(("seq", "head"), None)
    return jax.shard_map(local, mesh=mesh, in_specs=in_specs, out_specs=out_specs, check_vma=False)
```

```python
import functools
import math

import jax
import jax.numpy as jnp
from jax import lax
from jax.experimental import pallas as pl
from jax.experimental.pallas import tpu as pltpu
from jax.sharding import PartitionSpec as P

QH = 8
KVH = 4
HD = 256
NSEG = 64
BLK = 16
LANES = 128
EPSILON = 1e-06
SOFT_CAP = 50.0
FAR = 1073741824
VMEM_BYTES = 40 << 20


def rms_scale(matrix, scaling):
    matrix = matrix.astype(jnp.float32)
    mean_square = jnp.mean(matrix * matrix, axis=-1, keepdims=True)
    return matrix * lax.rsqrt(mean_square + EPSILON) * scaling


def frequencies(extent):
    return 10000.0 ** (-(jnp.arange(extent // 2, dtype=jnp.float32) * 2.0 / extent))


def turn(y, cosine, sine, scale):
    half = y.shape[1] // 2
    a, b = y[:, :half], y[:, half:]
    return (a * cosine - b * sine) * scale, (b * cosine + a * sine) * scale


def query_kernel(count, which_ref, cos_ref, sin_ref, w_ref, *rest):
    parts, out_ref = rest[:count], rest[count]
    half = HD // 2
    x = jnp.concatenate([part[...] for part in parts], axis=0)
    for h in range(w_ref.shape[1] // HD):
        y = jnp.dot(x, w_ref[:, h * HD : (h + 1) * HD], preferred_element_type=jnp.float32)
        a, b = turn(y, cos_ref[...], sin_ref[...], HD**-0.5)
        out_ref[h, :, :half] = a.astype(out_ref.dtype)
        out_ref[h, :, half:] = b.astype(out_ref.dtype)


def keyval_kernel(count, which_ref, cos_ref, sin_ref, w_ref, *rest):
    parts, out_ref = rest[:count], rest[count]
    half = HD // 2
    x = jnp.concatenate([part[...] for part in parts], axis=0)
    y = jnp.dot(x, w_ref[...], preferred_element_type=jnp.float32)
    a, b = turn(y[:, :HD], cos_ref[...], sin_ref[...], 1.0)
    out_ref[:, :half] = a.astype(out_ref.dtype)
    out_ref[:, half:HD] = b.astype(out_ref.dtype)
    out_ref[:, HD:] = y[:, HD:].astype(out_ref.dtype)


def project(body, parts, weight, columns, which, cosine, sine, out_shape):
    rows = cosine.shape[0]
    width = weight.shape[0]
    whole = [pl.BlockSpec(x.shape, lambda i, s: (0, 0)) for x in (cosine, sine)]
    return pl.pallas_call(
        functools.partial(body, len(parts)),
        grid_spec=pltpu.PrefetchScalarGridSpec(
            num_scalar_prefetch=1,
            grid=(1,),
            in_specs=whole
            + [pl.BlockSpec((width, columns), lambda i, s: (0, s[0]))]
            + [pl.BlockSpec(x.shape, lambda i, s: (0, 0)) for x in parts],
            out_specs=pl.BlockSpec(out_shape, lambda i, s: (0,) * len(out_shape)),
        ),
        out_shape=jax.ShapeDtypeStruct(out_shape, jnp.bfloat16),
        compiler_params=pltpu.CompilerParams(vmem_limit_bytes=VMEM_BYTES),
        cost_estimate=pl.CostEstimate(
            flops=2 * rows * width * columns,
            bytes_accessed=2 * width * (columns + rows),
            transcendentals=0,
        ),
        name="project",
    )(which.reshape(1), cosine, sine, weight, *parts)


def fold_blocks(
    heads, q_tile, k_tile, touch_ref, q_ref, qseg_ref, qslot_ref, kseg_ref, kslot_ref, parts, acc, den
):
    q_tiles = q_ref.shape[1] // q_tile
    blocks = kseg_ref.shape[0]
    first = 0
    for part in parts:
        here = part.shape[0] // k_tile

        def step(index, carry, part=part, here=here, first=first):
            qi = index // here
            kj = index % here

            @pl.when(touch_ref[qi * blocks + first + kj] > 0)
            def _():
                rows = pl.ds(pl.multiple_of(qi * q_tile, q_tile), q_tile)
                keys = pl.ds(pl.multiple_of(kj * k_tile, k_tile), k_tile)
                allowed = (kseg_ref[first + kj] == qseg_ref[rows, :]) & (
                    kslot_ref[first + kj] <= qslot_ref[rows, :]
                )
                for h in range(heads):
                    scores = lax.dot_general(
                        q_ref[h, rows, :],
                        part[keys, :HD],
                        (((1,), (1,)), ((), ())),
                        preferred_element_type=jnp.float32,
                    )
                    scores = jnp.tanh(scores * (1.0 / SOFT_CAP))
                    weights = jnp.where(
                        allowed, jnp.exp2(scores * (SOFT_CAP * math.log2(math.e))), 0.0
                    )
                    total = weights[:, :LANES]
                    for c in range(1, k_tile // LANES):
                        total += weights[:, c * LANES : (c + 1) * LANES]
                    den[h, rows, :] += total
                    acc[h, rows, :] += jnp.dot(
                        weights.astype(jnp.bfloat16),
                        part[keys, HD:],
                        preferred_element_type=jnp.float32,
                    )

            return carry

        lax.fori_loop(0, q_tiles * here, step, 0)
        first += here


def middle_kernel(heads, q_tile, k_tile, count, touch_ref, q_ref, qseg_ref, qslot_ref, kseg_ref, kslot_ref, *rest):
    parts, (acc_in, den_in, acc, den) = rest[:count], rest[count:]
    acc[...] = acc_in[...]
    den[...] = den_in[...]
    fold_blocks(
        heads, q_tile, k_tile, touch_ref, q_ref, qseg_ref, qslot_ref, kseg_ref, kslot_ref, parts, acc, den
    )


def first_kernel(heads, q_tile, k_tile, count, touch_ref, q_ref, qseg_ref, qslot_ref, kseg_ref, kslot_ref, *rest):
    parts, (acc, den) = rest[:count], rest[count:]
    acc[...] = jnp.zeros_like(acc)
    den[...] = jnp.zeros_like(den)
    fold_blocks(
        heads, q_tile, k_tile, touch_ref, q_ref, qseg_ref, qslot_ref, kseg_ref, kslot_ref, parts, acc, den
    )


def last_kernel(heads, q_tile, k_tile, count, touch_ref, q_ref, qseg_ref, qslot_ref, kseg_ref, kslot_ref, *rest):
    parts, (acc_in, den_in, out_ref, acc, den) = rest[:count], rest[count:]
    acc[...] = acc_in[...]
    den[...] = den_in[...]
    fold_blocks(
        heads, q_tile, k_tile, touch_ref, q_ref, qseg_ref, qslot_ref, kseg_ref, kslot_ref, parts, acc, den
    )
    present = qseg_ref[...] >= 0
    for h in range(heads):
        total = jnp.sum(den[h], axis=-1, keepdims=True)
        safe = jnp.where(present, total, 1.0)
        out_ref[:, h * HD : (h + 1) * HD] = jnp.where(present, acc[h] / safe, 0.0).astype(
            out_ref.dtype
        )


def attend(queries, q_seg, q_slot, parts, ints, totals=None, last=False):
    heads, rows, _ = queries.shape
    k_seg = jnp.concatenate([pair[0] for pair in ints])
    k_slot = jnp.concatenate([pair[1] for pair in ints])
    q_tile = math.gcd(rows, 256)
    k_tile = math.gcd(*[part.shape[0] for part in parts], 512)
    blocks = k_seg.shape[0] // k_tile
    seg_tiles = q_seg.reshape(-1, q_tile)
    lowest = jnp.min(jnp.where(seg_tiles >= 0, seg_tiles, FAR), axis=1)[:, None]
    highest = jnp.max(seg_tiles, axis=1)[:, None]
    latest = jnp.max(q_slot.reshape(-1, q_tile), axis=1)[:, None]
    near = (k_seg[None] >= lowest) & (k_seg[None] <= highest) & (k_slot[None] <= latest)
    touch = jnp.max(near.astype(jnp.int32).reshape(-1, blocks, k_tile), axis=2).reshape(-1)
    operands = [
        touch,
        queries,
        q_seg[:, None],
        q_slot[:, None],
        k_seg.reshape(blocks, 1, k_tile),
        k_slot.reshape(blocks, 1, k_tile),
        *parts,
    ]
    vmem = pl.BlockSpec(memory_space=pltpu.VMEM)
    sums = [
        jax.ShapeDtypeStruct((heads, rows, HD), jnp.float32),
        jax.ShapeDtypeStruct((heads, rows, LANES), jnp.float32),
    ]
    body, out_shape, out_specs, scratch = first_kernel, sums, [vmem, vmem], []
    if totals is not None:
        operands += list(totals)
        body = middle_kernel
    if last:
        body = last_kernel
        out_shape = jax.ShapeDtypeStruct((rows, heads * HD), jnp.bfloat16)
        out_specs = vmem
        scratch = [pltpu.VMEM(s.shape, s.dtype) for s in sums]
    pairs = heads * rows * k_seg.shape[0]
    return pl.pallas_call(
        functools.partial(body, heads, q_tile, k_tile, len(parts)),
        in_specs=[pl.BlockSpec(memory_space=pltpu.SMEM)] + [vmem] * (len(operands) - 1),
        out_specs=out_specs,
        out_shape=out_shape,
        scratch_shapes=scratch,
        compiler_params=pltpu.CompilerParams(vmem_limit_bytes=VMEM_BYTES),
        cost_estimate=pl.CostEstimate(
            flops=4 * pairs * HD, bytes_accessed=4 * HD * k_seg.shape[0], transcendentals=2 * pairs
        ),
        name="attend",
    )(*operands)


def local(
    tokens,
    in_gain,
    out_gain,
    query_weight,
    keyval_weight,
    out_weight,
    cache_entries,
    segment_ids,
    cache_lengths,
    block_owners,
):
    heads_here = query_weight.shape[1] // HD
    group_size = QH // KVH
    seq_size, head_size = lax.axis_size("seq"), lax.axis_size("head")
    seq_index = lax.axis_index("seq")
    head_index = lax.axis_index("head")
    shared_head = head_index * heads_here // group_size
    stream_rows = segment_ids.shape[0]
    own_rows = tokens.shape[0]
    square = head_size == 4

    def across(array, bits):
        return lax.ppermute(array, "head", [(h, h ^ bits) for h in range(head_size)])

    def relative(array):
        if not square:
            return array
        array = array.reshape(-1, 2, 2, own_rows)
        array = jnp.where(head_index % 2 == 1, array[:, :, ::-1], array)
        array = jnp.where(head_index // 2 == 1, array[:, ::-1], array)
        return array.reshape(-1)

    normed_own = rms_scale(tokens, in_gain).astype(jnp.bfloat16)
    if square:
        half = own_rows // 2
        from_x = across(normed_own, 1)
        from_y = across(normed_own, 2)
        diag_top = across(from_x[:half], 2)
        diag_bottom = across(from_y[half:], 1)
        chunks = [[normed_own, from_x], [from_y, diag_top, diag_bottom]]
    else:
        chunks = [[lax.all_gather(normed_own, "head", axis=0, tiled=True)]]

    cache_own = lax.dynamic_index_in_dim(cache_entries, shared_head, 0, keepdims=False)
    cache_pairs = lax.all_gather(cache_own, "seq", axis=0, tiled=True)

    table = jnp.concatenate([segment_ids, block_owners])[None]
    bits = 0
    while 1 << bits < seq_size:
        step = 1 << bits
        other = lax.ppermute(table, "seq", [(s, s ^ step) for s in range(seq_size)])
        table = jnp.concatenate([table, other], axis=0)
        bits += 1
    for bit in range(bits):
        pieces = table.reshape(-1, 2, 1 << bit, table.shape[-1])
        pieces = jnp.where((seq_index >> bit) % 2 == 1, pieces[:, ::-1], pieces)
        table = pieces.reshape(seq_size, -1)
    seg_all = table[:, :stream_rows].reshape(-1)
    owners = table[:, stream_rows:].reshape(-1)

    seg_range = jnp.arange(NSEG, dtype=jnp.int32)
    earlier = (seg_all[None, :] >= 0) & (seg_all[None, :] < seg_range[:, None])
    firsts = jnp.sum(earlier.astype(jnp.int32), axis=1)
    slots_all = jnp.arange(seg_all.shape[0], dtype=jnp.int32)
    seg_all, slots_all = relative(seg_all), relative(slots_all)
    begin = seq_index * stream_rows
    q_seg = lax.dynamic_slice_in_dim(seg_all, begin, stream_rows)
    q_slot = lax.dynamic_slice_in_dim(slots_all, begin, stream_rows)
    matches = (q_seg[:, None] == seg_range[None, :]).astype(jnp.int32)
    positions = jnp.sum(matches * (cache_lengths - firsts)[None, :], axis=1) + q_slot
    angles = positions.astype(jnp.float32)[:, None] * frequencies(HD)[None, :]
    cosine, sine = jnp.cos(angles), jnp.sin(angles)

    block_index = jnp.arange(owners.shape[0], dtype=jnp.int32)
    same = (owners[:, None] == owners[None, :]) & (block_index[None, :] < block_index[:, None])
    block_rank = jnp.sum(same.astype(jnp.int32), axis=1)
    owner_match = (owners[:, None] == seg_range[None, :]).astype(jnp.int32)
    limits = jnp.sum(owner_match * cache_lengths[None, :], axis=1)
    offsets = jnp.arange(BLK, dtype=jnp.int32)
    usable = (owners[:, None] >= 0) & (
        block_rank[:, None] * BLK + offsets[None, :] < limits[:, None]
    )
    cache_seg = jnp.where(usable, owners[:, None], -2).reshape(-1)
    cache_slot = jnp.full((cache_seg.shape[0],), -1, jnp.int32)

    chunk_rows = stream_rows // len(chunks)
    pairs = []
    for at, parts in enumerate(chunks):
        rows = slice(at * chunk_rows, (at + 1) * chunk_rows)
        pairs.append(
            project(
                keyval_kernel, parts, keyval_weight, 2 * HD, shared_head,
                cosine[rows], sine[rows], (chunk_rows, 2 * HD),
            )
        )
    queries = project(
        query_kernel, sum(chunks, []), query_weight, heads_here * HD, jnp.int32(0),
        cosine, sine, (heads_here, stream_rows, HD),
    )

    hops = seq_size // 4

    def onward(array):
        return lax.ppermute(array, "seq", [(s, s + 2) for s in range(seq_size - 2)])

    def sibling(array):
        return lax.ppermute(array, "seq", [(s, s ^ 1) for s in range(seq_size)])

    key_seg = jnp.where(seg_all >= 0, seg_all, -2)

    def shard_ints(shard):
        inside = (shard >= 0) & (shard < seq_size)
        at = jnp.clip(shard, 0, seq_size - 1) * stream_rows
        seg = lax.dynamic_slice_in_dim(key_seg, at, stream_rows)
        return jnp.where(inside, seg, -2), lax.dynamic_slice_in_dim(slots_all, at, stream_rows)

    mate = seq_index + 1 - 2 * (seq_index % 2)
    travelling = [onward(pair) for pair in pairs]
    waiting, waiting_ints = [sibling(pair) for pair in pairs], [shard_ints(mate)]
    totals = attend(
        queries, q_seg, q_slot, pairs + [cache_pairs], [shard_ints(seq_index), (cache_seg, cache_slot)]
    )
    for hop in range(1, hops + 1):
        travelling, totals = lax.optimization_barrier((travelling, totals))
        following = [onward(pair) for pair in travelling] if hop < hops else []
        beside = [sibling(pair) for pair in travelling]
        parts = waiting + travelling
        ints = waiting_ints + [shard_ints(seq_index - 2 * hop)]
        waiting, waiting_ints = beside, [shard_ints(mate - 2 * hop)]
        if hop < hops:
            totals = attend(queries, q_seg, q_slot, parts, ints, totals)
        else:
            attended = attend(
                queries, q_seg, q_slot, parts + waiting, ints + waiting_ints, totals, last=True
            )
        travelling = following

    if square:
        r = own_rows
        c = out_weight.shape[1] // 2
        left = jnp.dot(attended, out_weight[:, :c], preferred_element_type=jnp.float32)
        right = jnp.dot(attended, out_weight[:, c:], preferred_element_type=jnp.float32)
        wire = jnp.bfloat16
        send_l = jnp.concatenate([left[r : 2 * r], left[3 * r :]]).astype(wire)
        got_l = across(send_l, 1).astype(jnp.float32)
        got_r = across(right[2 * r :].astype(wire), 2).astype(jnp.float32)
        last_l = across((left[2 * r : 3 * r] + got_l[r:]).astype(wire), 2)
        last_r = across((right[r : 2 * r] + got_r[r:]).astype(wire), 1)
        branch = jnp.concatenate(
            [
                left[:r] + got_l[:r] + last_l.astype(jnp.float32),
                right[:r] + got_r[:r] + last_r.astype(jnp.float32),
            ],
            axis=1,
        )
    else:
        branch = lax.psum_scatter(
            jnp.dot(attended, out_weight, preferred_element_type=jnp.float32),
            "head",
            scatter_dimension=0,
            tiled=True,
        )
    return (tokens.astype(jnp.float32) + rms_scale(branch, out_gain)).astype(jnp.bfloat16)


def solution(mesh):
    in_specs = (
        P(("seq", "head"), None),
        P(),
        P(),
        P(None, "head"),
        P(),
        P("head", None),
        P(None, "seq", None),
        P("seq"),
        P(),
        P("seq"),
    )
    out_specs = P(("seq", "head"), None)
    return jax.shard_map(local, mesh=mesh, in_specs=in_specs, out_specs=out_specs, check_vma=False)
```

```python
import functools
import math

import jax
import jax.numpy as jnp
from jax import lax
from jax.experimental import pallas as pl
from jax.experimental.pallas import tpu as pltpu
from jax.sharding import PartitionSpec as P

QH = 8
KVH = 4
HD = 256
NSEG = 64
BLK = 16
LANES = 128
EPSILON = 1e-06
SOFT_CAP = 50.0
FAR = 1073741824
VMEM_BYTES = 40 << 20


def rms_scale(matrix, scaling):
    matrix = matrix.astype(jnp.float32)
    mean_square = jnp.mean(matrix * matrix, axis=-1, keepdims=True)
    return matrix * lax.rsqrt(mean_square + EPSILON) * scaling


def frequencies(extent):
    return 10000.0 ** (-(jnp.arange(extent // 2, dtype=jnp.float32) * 2.0 / extent))


def turn(y, cosine, sine, scale):
    half = y.shape[1] // 2
    a, b = y[:, :half], y[:, half:]
    return (a * cosine - b * sine) * scale, (b * cosine + a * sine) * scale


def query_kernel(count, which_ref, cos_ref, sin_ref, w_ref, *rest):
    parts, out_ref = rest[:count], rest[count]
    half = HD // 2
    x = jnp.concatenate([part[...] for part in parts], axis=0)
    for h in range(w_ref.shape[1] // HD):
        y = jnp.dot(x, w_ref[:, h * HD : (h + 1) * HD], preferred_element_type=jnp.float32)
        a, b = turn(y, cos_ref[...], sin_ref[...], HD**-0.5)
        out_ref[h, :, :half] = a.astype(out_ref.dtype)
        out_ref[h, :, half:] = b.astype(out_ref.dtype)


def keyval_kernel(count, which_ref, cos_ref, sin_ref, w_ref, *rest):
    parts, out_ref = rest[:count], rest[count]
    half = HD // 2
    x = jnp.concatenate([part[...] for part in parts], axis=0)
    y = jnp.dot(x, w_ref[...], preferred_element_type=jnp.float32)
    a, b = turn(y[:, :HD], cos_ref[...], sin_ref[...], 1.0)
    out_ref[:, :half] = a.astype(out_ref.dtype)
    out_ref[:, half:HD] = b.astype(out_ref.dtype)
    out_ref[:, HD:] = y[:, HD:].astype(out_ref.dtype)


def project(body, parts, weight, columns, which, cosine, sine, out_shape):
    rows = cosine.shape[0]
    width = weight.shape[0]
    whole = [pl.BlockSpec(x.shape, lambda i, s: (0, 0)) for x in (cosine, sine)]
    return pl.pallas_call(
        functools.partial(body, len(parts)),
        grid_spec=pltpu.PrefetchScalarGridSpec(
            num_scalar_prefetch=1,
            grid=(1,),
            in_specs=whole
            + [pl.BlockSpec((width, columns), lambda i, s: (0, s[0]))]
            + [pl.BlockSpec(x.shape, lambda i, s: (0, 0)) for x in parts],
            out_specs=pl.BlockSpec(out_shape, lambda i, s: (0,) * len(out_shape)),
        ),
        out_shape=jax.ShapeDtypeStruct(out_shape, jnp.bfloat16),
        compiler_params=pltpu.CompilerParams(vmem_limit_bytes=VMEM_BYTES),
        cost_estimate=pl.CostEstimate(
            flops=2 * rows * width * columns,
            bytes_accessed=2 * width * (columns + rows),
            transcendentals=0,
        ),
        name="project",
    )(which.reshape(1), cosine, sine, weight, *parts)


def fold_blocks(
    heads, q_tile, k_tile, touch_ref, q_ref, qseg_ref, qslot_ref, kseg_ref, kslot_ref, parts, acc, den
):
    q_tiles = q_ref.shape[1] // q_tile
    blocks = kseg_ref.shape[0]
    first = 0
    for part in parts:
        here = part.shape[0] // k_tile

        def step(index, carry, part=part, here=here, first=first):
            qi = index // here
            kj = index % here

            @pl.when(touch_ref[qi * blocks + first + kj] > 0)
            def _():
                rows = pl.ds(pl.multiple_of(qi * q_tile, q_tile), q_tile)
                keys = pl.ds(pl.multiple_of(kj * k_tile, k_tile), k_tile)
                allowed = (kseg_ref[first + kj] == qseg_ref[rows, :]) & (
                    kslot_ref[first + kj] <= qslot_ref[rows, :]
                )
                for h in range(heads):
                    scores = lax.dot_general(
                        q_ref[h, rows, :],
                        part[keys, :HD],
                        (((1,), (1,)), ((), ())),
                        preferred_element_type=jnp.float32,
                    )
                    scores = jnp.tanh(scores * (1.0 / SOFT_CAP))
                    weights = jnp.where(
                        allowed, jnp.exp2(scores * (SOFT_CAP * math.log2(math.e))), 0.0
                    )
                    total = weights[:, :LANES]
                    for c in range(1, k_tile // LANES):
                        total += weights[:, c * LANES : (c + 1) * LANES]
                    den[h, rows, :] += total
                    acc[h, rows, :] += jnp.dot(
                        weights.astype(jnp.bfloat16),
                        part[keys, HD:],
                        preferred_element_type=jnp.float32,
                    )

            return carry

        lax.fori_loop(0, q_tiles * here, step, 0)
        first += here


def middle_kernel(heads, q_tile, k_tile, count, touch_ref, q_ref, qseg_ref, qslot_ref, kseg_ref, kslot_ref, *rest):
    parts, (acc_in, den_in, acc, den) = rest[:count], rest[count:]
    acc[...] = acc_in[...]
    den[...] = den_in[...]
    fold_blocks(
        heads, q_tile, k_tile, touch_ref, q_ref, qseg_ref, qslot_ref, kseg_ref, kslot_ref, parts, acc, den
    )


def first_kernel(heads, q_tile, k_tile, count, touch_ref, q_ref, qseg_ref, qslot_ref, kseg_ref, kslot_ref, *rest):
    parts, (acc, den) = rest[:count], rest[count:]
    acc[...] = jnp.zeros_like(acc)
    den[...] = jnp.zeros_like(den)
    fold_blocks(
        heads, q_tile, k_tile, touch_ref, q_ref, qseg_ref, qslot_ref, kseg_ref, kslot_ref, parts, acc, den
    )


def last_kernel(heads, q_tile, k_tile, count, touch_ref, q_ref, qseg_ref, qslot_ref, kseg_ref, kslot_ref, *rest):
    parts, (acc_in, den_in, out_ref, acc, den) = rest[:count], rest[count:]
    acc[...] = acc_in[...]
    den[...] = den_in[...]
    fold_blocks(
        heads, q_tile, k_tile, touch_ref, q_ref, qseg_ref, qslot_ref, kseg_ref, kslot_ref, parts, acc, den
    )
    present = qseg_ref[...] >= 0
    for h in range(heads):
        total = jnp.sum(den[h], axis=-1, keepdims=True)
        safe = jnp.where(present, total, 1.0)
        out_ref[:, h * HD : (h + 1) * HD] = jnp.where(present, acc[h] / safe, 0.0).astype(
            out_ref.dtype
        )


def attend(queries, q_seg, q_slot, parts, ints, totals=None, last=False):
    heads, rows, _ = queries.shape
    k_seg = jnp.concatenate([pair[0] for pair in ints])
    k_slot = jnp.concatenate([pair[1] for pair in ints])
    q_tile = math.gcd(rows, 256)
    k_tile = math.gcd(*[part.shape[0] for part in parts], 512)
    blocks = k_seg.shape[0] // k_tile
    seg_tiles = q_seg.reshape(-1, q_tile)
    lowest = jnp.min(jnp.where(seg_tiles >= 0, seg_tiles, FAR), axis=1)[:, None]
    highest = jnp.max(seg_tiles, axis=1)[:, None]
    latest = jnp.max(q_slot.reshape(-1, q_tile), axis=1)[:, None]
    near = (k_seg[None] >= lowest) & (k_seg[None] <= highest) & (k_slot[None] <= latest)
    touch = jnp.max(near.astype(jnp.int32).reshape(-1, blocks, k_tile), axis=2).reshape(-1)
    operands = [
        touch,
        queries,
        q_seg[:, None],
        q_slot[:, None],
        k_seg.reshape(blocks, 1, k_tile),
        k_slot.reshape(blocks, 1, k_tile),
        *parts,
    ]
    vmem = pl.BlockSpec(memory_space=pltpu.VMEM)
    sums = [
        jax.ShapeDtypeStruct((heads, rows, HD), jnp.float32),
        jax.ShapeDtypeStruct((heads, rows, LANES), jnp.float32),
    ]
    body, out_shape, out_specs, scratch = first_kernel, sums, [vmem, vmem], []
    if totals is not None:
        operands += list(totals)
        body = middle_kernel
    if last:
        body = last_kernel
        out_shape = jax.ShapeDtypeStruct((rows, heads * HD), jnp.bfloat16)
        out_specs = vmem
        scratch = [pltpu.VMEM(s.shape, s.dtype) for s in sums]
    pairs = heads * rows * k_seg.shape[0]
    return pl.pallas_call(
        functools.partial(body, heads, q_tile, k_tile, len(parts)),
        in_specs=[pl.BlockSpec(memory_space=pltpu.SMEM)] + [vmem] * (len(operands) - 1),
        out_specs=out_specs,
        out_shape=out_shape,
        scratch_shapes=scratch,
        compiler_params=pltpu.CompilerParams(vmem_limit_bytes=VMEM_BYTES),
        cost_estimate=pl.CostEstimate(
            flops=4 * pairs * HD, bytes_accessed=4 * HD * k_seg.shape[0], transcendentals=2 * pairs
        ),
        name="attend",
    )(*operands)


def local(
    tokens,
    in_gain,
    out_gain,
    query_weight,
    keyval_weight,
    out_weight,
    cache_entries,
    segment_ids,
    cache_lengths,
    block_owners,
):
    heads_here = query_weight.shape[1] // HD
    group_size = QH // KVH
    seq_size, head_size = lax.axis_size("seq"), lax.axis_size("head")
    seq_index = lax.axis_index("seq")
    head_index = lax.axis_index("head")
    shared_head = head_index * heads_here // group_size
    stream_rows = segment_ids.shape[0]
    own_rows = tokens.shape[0]
    square = head_size == 4

    def across(array, bits):
        return lax.ppermute(array, "head", [(h, h ^ bits) for h in range(head_size)])

    def relative(array):
        if not square:
            return array
        array = array.reshape(-1, 2, 2, own_rows)
        array = jnp.where(head_index % 2 == 1, array[:, :, ::-1], array)
        array = jnp.where(head_index // 2 == 1, array[:, ::-1], array)
        return array.reshape(-1)

    normed_own = rms_scale(tokens, in_gain).astype(jnp.bfloat16)
    if square:
        half = own_rows // 2
        from_x = across(normed_own, 1)
        from_y = across(normed_own, 2)
        diag_top = across(from_x[:half], 2)
        diag_bottom = across(from_y[half:], 1)
        chunks = [[normed_own, from_x], [from_y, diag_top, diag_bottom]]
    else:
        chunks = [[lax.all_gather(normed_own, "head", axis=0, tiled=True)]]

    cache_own = lax.dynamic_index_in_dim(cache_entries, shared_head, 0, keepdims=False)
    cache_pairs = lax.all_gather(cache_own, "seq", axis=0, tiled=True)

    table = jnp.concatenate([segment_ids, block_owners])[None]
    bits = 0
    while 1 << bits < seq_size:
        step = 1 << bits
        other = lax.ppermute(table, "seq", [(s, s ^ step) for s in range(seq_size)])
        table = jnp.concatenate([table, other], axis=0)
        bits += 1
    for bit in range(bits):
        pieces = table.reshape(-1, 2, 1 << bit, table.shape[-1])
        pieces = jnp.where((seq_index >> bit) % 2 == 1, pieces[:, ::-1], pieces)
        table = pieces.reshape(seq_size, -1)
    seg_all = table[:, :stream_rows].reshape(-1)
    owners = table[:, stream_rows:].reshape(-1)

    seg_range = jnp.arange(NSEG, dtype=jnp.int32)
    earlier = (seg_all[None, :] >= 0) & (seg_all[None, :] < seg_range[:, None])
    firsts = jnp.sum(earlier.astype(jnp.int32), axis=1)
    slots_all = jnp.arange(seg_all.shape[0], dtype=jnp.int32)
    seg_all, slots_all = relative(seg_all), relative(slots_all)
    begin = seq_index * stream_rows
    q_seg = lax.dynamic_slice_in_dim(seg_all, begin, stream_rows)
    q_slot = lax.dynamic_slice_in_dim(slots_all, begin, stream_rows)
    matches = (q_seg[:, None] == seg_range[None, :]).astype(jnp.int32)
    positions = jnp.sum(matches * (cache_lengths - firsts)[None, :], axis=1) + q_slot
    angles = positions.astype(jnp.float32)[:, None] * frequencies(HD)[None, :]
    cosine, sine = jnp.cos(angles), jnp.sin(angles)

    block_index = jnp.arange(owners.shape[0], dtype=jnp.int32)
    same = (owners[:, None] == owners[None, :]) & (block_index[None, :] < block_index[:, None])
    block_rank = jnp.sum(same.astype(jnp.int32), axis=1)
    owner_match = (owners[:, None] == seg_range[None, :]).astype(jnp.int32)
    limits = jnp.sum(owner_match * cache_lengths[None, :], axis=1)
    offsets = jnp.arange(BLK, dtype=jnp.int32)
    usable = (owners[:, None] >= 0) & (
        block_rank[:, None] * BLK + offsets[None, :] < limits[:, None]
    )
    cache_seg = jnp.where(usable, owners[:, None], -2).reshape(-1)
    cache_slot = jnp.full((cache_seg.shape[0],), -1, jnp.int32)

    w_shared = lax.dynamic_slice_in_dim(keyval_weight, shared_head * 2 * HD, 2 * HD, 1)
    chunk_rows = stream_rows // len(chunks)
    pairs = []
    for at, parts in enumerate(chunks):
        rows = slice(at * chunk_rows, (at + 1) * chunk_rows)
        pairs.append(
            project(
                keyval_kernel, parts, w_shared, 2 * HD, jnp.int32(0),
                cosine[rows], sine[rows], (chunk_rows, 2 * HD),
            )
        )
    queries = project(
        query_kernel, sum(chunks, []), query_weight, heads_here * HD, jnp.int32(0),
        cosine, sine, (heads_here, stream_rows, HD),
    )

    hops = seq_size // 4

    def onward(array):
        return lax.ppermute(array, "seq", [(s, s + 2) for s in range(seq_size - 2)])

    def sibling(array):
        return lax.ppermute(array, "seq", [(s, s ^ 1) for s in range(seq_size)])

    key_seg = jnp.where(seg_all >= 0, seg_all, -2)

    def shard_ints(shard):
        inside = (shard >= 0) & (shard < seq_size)
        at = jnp.clip(shard, 0, seq_size - 1) * stream_rows
        seg = lax.dynamic_slice_in_dim(key_seg, at, stream_rows)
        return jnp.where(inside, seg, -2), lax.dynamic_slice_in_dim(slots_all, at, stream_rows)

    mate = seq_index + 1 - 2 * (seq_index % 2)
    travelling = [onward(pair) for pair in pairs]
    waiting, waiting_ints = [sibling(pair) for pair in pairs], [shard_ints(mate)]
    totals = attend(
        queries, q_seg, q_slot, pairs + [cache_pairs], [shard_ints(seq_index), (cache_seg, cache_slot)]
    )
    for hop in range(1, hops + 1):
        travelling, totals = lax.optimization_barrier((travelling, totals))
        following = [onward(pair) for pair in travelling] if hop < hops else []
        beside = [sibling(pair) for pair in travelling]
        parts = waiting + travelling
        ints = waiting_ints + [shard_ints(seq_index - 2 * hop)]
        waiting, waiting_ints = beside, [shard_ints(mate - 2 * hop)]
        if hop < hops:
            totals = attend(queries, q_seg, q_slot, parts, ints, totals)
        else:
            attended = attend(
                queries, q_seg, q_slot, parts + waiting, ints + waiting_ints, totals, last=True
            )
        travelling = following

    if square:
        r = own_rows
        c = out_weight.shape[1] // 2
        left = jnp.dot(attended, out_weight[:, :c], preferred_element_type=jnp.float32)
        right = jnp.dot(attended, out_weight[:, c:], preferred_element_type=jnp.float32)
        wire = jnp.bfloat16
        send_l = jnp.concatenate([left[r : 2 * r], left[3 * r :]]).astype(wire)
        got_l = across(send_l, 1).astype(jnp.float32)
        got_r = across(right[2 * r :].astype(wire), 2).astype(jnp.float32)
        last_l = across((left[2 * r : 3 * r] + got_l[r:]).astype(wire), 2)
        last_r = across((right[r : 2 * r] + got_r[r:]).astype(wire), 1)
        branch = jnp.concatenate(
            [
                left[:r] + got_l[:r] + last_l.astype(jnp.float32),
                right[:r] + got_r[:r] + last_r.astype(jnp.float32),
            ],
            axis=1,
        )
    else:
        branch = lax.psum_scatter(
            jnp.dot(attended, out_weight, preferred_element_type=jnp.float32),
            "head",
            scatter_dimension=0,
            tiled=True,
        )
    return (tokens.astype(jnp.float32) + rms_scale(branch, out_gain)).astype(jnp.bfloat16)


def solution(mesh):
    in_specs = (
        P(("seq", "head"), None),
        P(),
        P(),
        P(None, "head"),
        P(),
        P("head", None),
        P(None, "seq", None),
        P("seq"),
        P(),
        P("seq"),
    )
    out_specs = P(("seq", "head"), None)
    return jax.shard_map(local, mesh=mesh, in_specs=in_specs, out_specs=out_specs, check_vma=False)
```
